512 devices in a mesh: vox: 64 (over x, y, core), grp: 8 (over z).
Axes of the slice: x: 4, y: 8, z: 8, core: 2. Of those that a mesh axis runs over, the one named last changes fastest.
Arguments:
- source_field: bfloat16 [1024, 65536], P(None, 'vox'), may hold values from -4 to 4
- detector_field: bfloat16 [1024, 65536], P(None, 'vox'), may hold values from -4 to 4
- active_block_pairs: int32 [256, 2], P('grp'), may hold values from 0 to 15, as said below
- measurement_counts: int32 [256], P('grp'), may hold values from 1 to 64
- measurement_residual: bfloat16 [256, 4096], P('grp'), may hold values from -6 to 6
Outputs:
- update: float32 [128, 512], P('vox')
- residual: float32 [128, 512], P('vox')
The draws below stay inside these ranges and needn't reach their ends.
Inputs may be any that keep to these rules, and one draw needn't show every extreme that they name: `active_block_pairs`: each row names a source block below 16 and a detector block below 16; no pair of blocks appears twice.
All inputs are finite; a program needn't handle non-finite values.
Results may differ from the reference program's by a relative error of at most 0.025.
Values may be sent and summed in bfloat16 or wider, within the bound.
A program may use at most 64 MiB of HBM per device.

```python
import math
import jax
import jax.numpy as jnp
from jax import lax

BLOCK_WIDTH = 64
SBLK = 16
DBLK = 16
NY = 32
NZ = 16
ITERS = 2
NX = 128
VOXELS = 65536
NSRC = 1024
NDET = 1024
PAIR_TOTAL = 256


def sensitivity(seed_key, row_count):
    depth_frac = (jnp.arange(VOXELS) // (NY * NZ)).astype(jnp.float32) / NX
    decay_rate = 0.7
    values = jax.random.truncated_normal(seed_key, -4.0, 4.0, (row_count, VOXELS), jnp.float32)
    return values * jnp.exp(-decay_rate * depth_frac)[None, :]


def draw_source_field(key, part):
    return sensitivity(jax.random.fold_in(key, 11), NSRC).astype(jnp.bfloat16)


def draw_detector_field(key, part):
    return sensitivity(jax.random.fold_in(key, 12), NDET).astype(jnp.bfloat16)


def draw_active_block_pairs(key, part):
    chosen = jax.random.permutation(jax.random.fold_in(key, 13), SBLK * DBLK)[:PAIR_TOTAL]
    return jnp.stack([chosen // DBLK, chosen % DBLK], axis=1).astype(jnp.int32)


def set_ends(entries, rng, low, top_value):
    shape = entries.shape
    index_at = [jax.random.randint(jax.random.fold_in(rng, axis), (), 0, shape[axis]) for axis in range(len(shape))]
    entries = entries.at[tuple(index_at)].set(low)
    longest = shape.index(max(shape))
    index_at[longest] = (index_at[longest] + 1) % shape[longest]
    return entries.at[tuple(index_at)].set(top_value)


def steps_of(own_key, shape, split, smallest, top_value):
    level = 1.0
    for position, parts in split:
        heights = jax.random.uniform(jax.random.fold_in(jax.random.fold_in(own_key, 6), position), (parts,), jnp.float32, smallest / len(split), top_value / len(split))
        level = level * jnp.repeat(jnp.exp(heights), shape[position] // parts).reshape((-1,) + (1,) * (len(shape) - 1 - position))
    return level


def normal_values(stream_key, extent, scale, bound, shards=(), held_as=jnp.bfloat16):
    values = scale * jax.random.normal(stream_key, extent, jnp.float32)
    if shards:
        values = values * steps_of(stream_key, extent, shards, -0.22, 0.18)
    return jnp.clip(values, -bound, bound).astype(held_as)


def setup_inputs(seed: int = 0) -> dict:
    seeds = jax.random.split(jax.random.key(seed), 6)
    source_field = draw_source_field(jax.random.fold_in(seeds[5], 71), 0)
    detector_field = draw_detector_field(jax.random.fold_in(seeds[5], 71), 0)
    active_block_pairs = draw_active_block_pairs(jax.random.fold_in(seeds[5], 71), 0)
    measurement_counts = set_ends(jax.random.randint(seeds[3], (PAIR_TOTAL,), 1, BLOCK_WIDTH + 1), jax.random.fold_in(seeds[3], 1), 1, BLOCK_WIDTH).astype(jnp.int32)
    measurement_residual = normal_values(seeds[4], (PAIR_TOTAL, BLOCK_WIDTH * BLOCK_WIDTH), 1.0, 6.0, ((0, 8),))
    return dict(source_field=source_field, detector_field=detector_field, active_block_pairs=active_block_pairs, measurement_counts=measurement_counts, measurement_residual=measurement_residual)


reg_weight = 0.1

def laplace_term(voxel_field):
    grid_cube = voxel_field.reshape(NX, NY, NZ)
    padded = jnp.pad(grid_cube, 1)
    beside = padded[2:, 1:-1, 1:-1] + padded[:-2, 1:-1, 1:-1]
    beside = beside + padded[1:-1, 2:, 1:-1] + padded[1:-1, :-2, 1:-1]
    beside = beside + padded[1:-1, 1:-1, 2:] + padded[1:-1, 1:-1, :-2]
    return (7.0 * grid_cube - beside).reshape(NX, NY * NZ)

def reference(source_field, detector_field, active_block_pairs, measurement_counts, measurement_residual):
    norm_factor = 1.0 / math.sqrt(PAIR_TOTAL * BLOCK_WIDTH * BLOCK_WIDTH)
    column_entry = jnp.arange(BLOCK_WIDTH * BLOCK_WIDTH, dtype=jnp.int32) % BLOCK_WIDTH
    measurement_mask = (column_entry[None, :] < measurement_counts[:, None]).astype(jnp.float32)

    def block_of(whole_field, block_id):
        return lax.dynamic_slice_in_dim(whole_field, (block_id * BLOCK_WIDTH).astype(jnp.int32), BLOCK_WIDTH, 0)

    def measure(direction):
        flattened = direction.reshape(-1)

        def one_pair(pair_row):
            source_rows = block_of(source_field, pair_row[0]).astype(jnp.float32)
            detect_rows = block_of(detector_field, pair_row[1])
            scaled = (source_rows * flattened[None, :]).astype(jnp.bfloat16)
            product = jnp.dot(scaled, detect_rows.T, preferred_element_type=jnp.float32)
            return norm_factor * product.reshape(-1)
        measured = lax.map(one_pair, active_block_pairs)
        return (measurement_mask * measured).astype(jnp.bfloat16)

    def project_backward(weights):

        def accumulate(running, pair_item):
            pair_row, weight_row = pair_item
            source_rows = block_of(source_field, pair_row[0]).astype(jnp.float32)
            detect_rows = block_of(detector_field, pair_row[1])
            spread = jnp.dot(weight_row.reshape(BLOCK_WIDTH, BLOCK_WIDTH), detect_rows, preferred_element_type=jnp.float32)
            return (running + lax.optimization_barrier(jnp.sum(source_rows * spread, axis=0)), None)
        running, unused_out = lax.scan(accumulate, jnp.zeros((VOXELS,), jnp.float32), (active_block_pairs, weights))
        return (norm_factor * running).reshape(NX, NY * NZ)

    def operate(direction):
        return project_backward(measure(direction)) + reg_weight * laplace_term(direction)
    right_hand_side = project_backward((measurement_mask * measurement_residual).astype(jnp.bfloat16))
    update = jnp.zeros_like(right_hand_side)
    residual = right_hand_side
    direction = right_hand_side
    norm_now = jnp.sum(residual * residual)
    for iteration in range(ITERS):
        applied = operate(direction)
        step_length = norm_now / jnp.sum(direction * applied)
        update = update + step_length * direction
        residual = residual - step_length * applied
        norm_next = jnp.sum(residual * residual)
        direction = residual + norm_next / norm_now * direction
        norm_now = norm_next
    return (update, residual)
```

```python
import functools

import jax
import jax.numpy as jnp
from jax import lax
from jax.experimental import pallas as pl
from jax.experimental.pallas import tpu as pltpu
from jax.sharding import PartitionSpec as P

MESH = pl.DeviceIdType.MESH
F32 = jnp.float32
BF16 = jnp.bfloat16

BLOCK = 64
NORM = 1.0 / 1024.0
REG = 0.1
CHIPS = 32
PLANES = 8
PAIRS = 32


def dot_nt(a, b):
    return lax.dot_general(a, b, (((1,), (1,)), ((), ())), preferred_element_type=F32)


def dot_nn(a, b):
    return lax.dot_general(a, b, (((1,), (0,)), ((), ())), preferred_element_type=F32)


def lane_sum(row):
    return jnp.sum(row, axis=1, keepdims=True)


def fold_rows(acc):
    out = []
    for j in range(8):
        out.append(jnp.sum(acc[:, j * 128 : (j + 1) * 128], axis=0, keepdims=True))
    return NORM * jnp.concatenate(out, axis=0)


def right_side_kernel(pairs, counts, s_ref, d_ref, r_ref, back, zrow, acc):
    vox = lax.axis_index("vox")
    m = vox // 2
    c = vox % 2
    row8 = lax.broadcasted_iota(jnp.int32, (8, 128), 0)
    lane8 = lax.broadcasted_iota(jnp.int32, (8, 128), 1)

    t_own = c * 8 + (m % 4) * 2 + lane8 // BLOCK
    s_own = 2 * row8 + m // 16

    def add_count(p, total):
        hit = (s_own == pairs[p, 0]) & (t_own == pairs[p, 1])
        return total + jnp.where(hit, counts[p].astype(F32), 0.0)

    count_rows = lax.fori_loop(0, PAIRS, add_count, jnp.zeros((8, 128), F32))
    for z in range(PLANES):
        zrow[z] = count_rows[z : z + 1, :]

    lane64 = lax.broadcasted_iota(jnp.int32, (BLOCK, 128), 1)
    acc[...] = jnp.zeros_like(acc)

    def four_pairs(q, carry):
        ids = [4 * q + i for i in range(4)]
        zero = jnp.zeros((BLOCK, 128), BF16)
        rows = []
        for half in range(2):
            low, high = counts[ids[2 * half]], counts[ids[2 * half + 1]]
            block = r_ref[2 * q + half].astype(F32)
            keep_low = lane64 < low
            keep_high = (lane64 >= BLOCK) & (lane64 - BLOCK < high)
            low_part = jnp.where(keep_low & (lane64 < BLOCK), block, 0.0).astype(BF16)
            high_part = jnp.where(keep_high, block, 0.0).astype(BF16)
            for part in (low_part, high_part):
                rows.append(jnp.concatenate([part, zero] if half == 0 else [zero, part], axis=1))
        lhs = jnp.concatenate(rows, axis=0)
        s_at = [pl.multiple_of(pairs[i, 0] * BLOCK, BLOCK) for i in ids]
        t_at = [pl.multiple_of(pairs[i, 1] * BLOCK, BLOCK) for i in ids]
        for n in range(4):
            cols = slice(n * 256, (n + 1) * 256)
            rhs = jnp.concatenate([d_ref[pl.ds(at, BLOCK), cols] for at in t_at], axis=0)
            src = jnp.concatenate([s_ref[pl.ds(at, BLOCK), cols] for at in s_at], axis=0)
            prod = dot_nn(lhs, rhs) * src.astype(F32)
            acc[:, cols] += jnp.sum(prod.reshape(32, 8, 256), axis=0)
        return carry

    lax.fori_loop(0, PAIRS // 4, four_pairs, 0)

    back[...] = fold_rows(acc)


def step_kernel(
    s_ref, d_ref, b_part, zrow,
    upd, res,
    scaled, acc, psend, prcv, pown, xsend, rs, w_all,
    vbuf, halo, csc_snd, csc_rcv, sc_snd, sc_rcv, zbuf, zsm,
    halo_s, halo_r, core_s, core_r, csc_s, csc_r, rs_s, rs_r, sc_s, sc_r,
    ag_s, ag_r, cw_s, cw_r, z_s, z_r, zsm_s, zsm_r,
):
    vox = lax.axis_index("vox")
    g = lax.axis_index("grp")
    m = vox // 2
    c = vox % 2
    partner = (vox + 1 - 2 * c, g)
    up = ((vox + 1) % 64, g)
    down = ((vox + 63) % 64, g)
    cross = ((vox + 63 + 2 * c) % 64, g)

    barrier = pltpu.get_barrier_semaphore()

    def chip_peer(k):
        return (m + k) % CHIPS

    def chip_device(peer):
        return (peer * 2 + c, g)

    def greet_chip(k, carry):
        pl.semaphore_signal(barrier, inc=1, device_id=chip_device(chip_peer(k)), device_id_type=MESH)
        return carry

    def greet_plane(k, carry):
        pl.semaphore_signal(barrier, inc=1, device_id=(vox, (g + k) % PLANES), device_id_type=MESH)
        return carry

    lax.fori_loop(1, PLANES, greet_plane, 0)
    pl.semaphore_signal(barrier, inc=1, device_id=partner, device_id_type=MESH)
    pl.semaphore_signal(barrier, inc=1, device_id=cross, device_id_type=MESH)
    lax.fori_loop(1, CHIPS, greet_chip, 0)

    def remote(src, dst, send, recv, device):
        return pltpu.make_async_remote_copy(
            src_ref=src, dst_ref=dst, send_sem=send, recv_sem=recv,
            device_id=device, device_id_type=MESH,
        )

    def drain(ref, sem):
        pltpu.make_async_copy(ref, ref, sem).wait()

    row8 = lax.broadcasted_iota(jnp.int32, (8, 128), 0)
    lane8 = lax.broadcasted_iota(jnp.int32, (8, 128), 1)

    pl.semaphore_wait(barrier, CHIPS - 1 + PLANES - 1 + 2)

    def plane_sum(phase, part, per_target):
        zbuf[phase, g] = part
        if per_target:
            zsm[phase, g] = zrow[g]

        def send(k, carry):
            peer = (g + k) % PLANES
            device = (vox, peer)
            mine = zbuf.at[phase, g]
            remote(mine, mine, z_s.at[phase], z_r.at[phase], device).start()
            small = zrow.at[peer] if per_target else zsm.at[phase, g]
            remote(small, zsm.at[phase, g], zsm_s.at[phase], zsm_r.at[phase], device).start()
            return carry

        lax.fori_loop(1, PLANES, send, 0)
        drain(zbuf.at[phase, pl.ds(0, PLANES - 1)], z_r.at[phase])
        drain(zsm.at[phase, pl.ds(0, PLANES - 1)], zsm_r.at[phase])
        return jnp.sum(zbuf[phase], axis=0), jnp.sum(zsm[phase], axis=0)

    def laplace(v, low, high):
        low = jnp.where(vox > 0, low, 0.0)
        high = jnp.where(vox < 63, high, 0.0)
        x_m = jnp.where(row8 < 4, pltpu.roll(low, 4, 0), pltpu.roll(v, 4, 0))
        x_p = jnp.where(row8 < 4, pltpu.roll(v, 4, 0), pltpu.roll(high, 4, 0))
        back = pltpu.roll(v, 16, 1)
        ahead = pltpu.roll(v, 112, 1)
        y_m = jnp.where(lane8 >= 16, back, jnp.where(row8 % 4 != 0, pltpu.roll(back, 1, 0), 0.0))
        y_p = jnp.where(lane8 < 112, ahead, jnp.where(row8 % 4 != 3, pltpu.roll(ahead, 7, 0), 0.0))
        z_m = jnp.where(lane8 % 16 != 0, pltpu.roll(v, 1, 1), 0.0)
        z_p = jnp.where(lane8 % 16 != 15, pltpu.roll(v, 127, 1), 0.0)
        return 7.0 * v - (x_m + x_p + y_m + y_p + z_m + z_p)

    s_rows = pl.ds(pl.multiple_of(g * 128, 128), 128)
    lt_own = m % 4
    row_own = pl.multiple_of((m // 4) * 16, 16)

    def forward(it, v, scalar_terms):
        vbuf[it] = v
        to_up = remote(vbuf.at[it], halo.at[it, 0], halo_s.at[it, 0], halo_r.at[it, 0], up)
        to_down = remote(vbuf.at[it], halo.at[it, 1], halo_s.at[it, 1], halo_r.at[it, 1], down)
        to_up.start()
        to_down.start()
        for j in range(8):
            cols = slice(j * 128, (j + 1) * 128)
            scaled[:, cols] = (s_ref[s_rows, cols].astype(F32) * v[j : j + 1, :]).astype(BF16)

        def half(side, n):
            start = pl.multiple_of(side * 512 + n * 256, 256)
            return dot_nt(scaled[...], d_ref[pl.ds(start, 256), :])

        for n in range(2):
            part = half(1 - c, n).astype(BF16)
            psend[it, 2 * n] = part[:, :128]
            psend[it, 2 * n + 1] = part[:, 128:]
        to_core = remote(psend.at[it], prcv.at[it], core_s.at[it], core_r.at[it], partner)
        to_core.start()

        to_up.wait()
        to_down.wait()
        lap = laplace(v, halo[it, 0], halo[it, 1])
        terms = scalar_terms(lap)
        packed = jnp.zeros((1, 128), F32)
        lane1 = lax.broadcasted_iota(jnp.int32, (1, 128), 1)
        for i, term in enumerate(terms):
            packed += jnp.where(lane1 == i, lane_sum(jnp.sum(term, axis=0, keepdims=True)), 0.0)
        csc_snd[it] = packed
        to_core_sc = remote(csc_snd.at[it], csc_rcv.at[it], csc_s.at[it], csc_r.at[it], partner)
        to_core_sc.start()

        for n in range(2):
            part = half(c, n)
            pown[2 * n] = part[:, :128]
            pown[2 * n + 1] = part[:, 128:]
        to_core.wait()
        for lt in range(4):
            total = pown[lt] + prcv[it, lt].astype(F32)
            pown[lt] = total
            xsend[it, lt] = total.astype(BF16)

        def scatter(k, carry):
            peer = chip_peer(k)
            src = xsend.at[it, peer % 4, pl.ds(pl.multiple_of((peer // 4) * 16, 16), 16), :]
            remote(src, rs.at[it, k - 1], rs_s.at[it], rs_r.at[it], chip_device(peer)).start()
            return carry

        lax.fori_loop(1, CHIPS, scatter, 0)

        to_core_sc.wait()
        mine = packed + csc_rcv[it]
        sc_snd[it] = mine

        def scatter_sc(k, carry):
            remote(
                sc_snd.at[it], sc_rcv.at[it, k - 1], sc_s.at[it], sc_r.at[it], chip_device(chip_peer(k))
            ).start()
            return carry

        lax.fori_loop(1, CHIPS, scatter_sc, 0)
        drain(rs.at[it], rs_r.at[it])
        total = pown[lt_own, pl.ds(row_own, 16), :] + jnp.sum(rs[it].astype(F32), axis=0)
        drain(sc_rcv.at[it], sc_r.at[it])
        sums = mine + jnp.sum(sc_rcv[it], axis=0)
        scalars = [lane_sum(jnp.where(lane1 == i, sums, 0.0)) for i in range(len(terms))]
        return NORM * total, scalars, lap

    def backward(it, weights):
        chunk = w_all.at[it, c * 4 + lt_own, pl.ds(row_own, 16), :]
        chunk[...] = weights

        def gather(k, carry):
            remote(chunk, chunk, ag_s.at[it], ag_r.at[it], chip_device(chip_peer(k))).start()
            return carry

        lax.fori_loop(1, CHIPS, gather, 0)
        drain(rs.at[it], ag_r.at[it])
        own_half = w_all.at[it, pl.ds(c * 4, 4)]
        to_core = remote(own_half, own_half, cw_s.at[it], cw_r.at[it], partner)
        to_core.start()
        acc[...] = jnp.zeros_like(acc)

        def use(side):
            tiles = w_all[it, pl.ds(side * 4, 4)]
            lhs = jnp.concatenate([tiles[i] for i in range(4)], axis=1)
            rows = pl.ds(pl.multiple_of(side * 512, 512), 512)
            for n in range(4):
                cols = slice(n * 256, (n + 1) * 256)
                prod = dot_nn(lhs, d_ref[rows, cols]) * s_ref[s_rows, cols].astype(F32)
                acc[:, cols] += jnp.sum(prod.reshape(16, 8, 256), axis=0)
            wide = tiles.astype(F32)
            return jnp.sum((wide * wide).reshape(64, 8, 128), axis=0)

        ww = use(c)
        to_core.wait()
        ww = ww + use(1 - c)
        zsm[it + 1, g] = jnp.sum(ww, axis=0, keepdims=True)
        back, ww_row = plane_sum(it + 1, fold_rows(acc), False)
        return back, lane_sum(ww_row)

    b, count_row = plane_sum(0, b_part[...], True)
    lane16 = lax.broadcasted_iota(jnp.int32, (16, 128), 1)
    keep = (lane16 % BLOCK).astype(F32) < count_row

    def masked(values):
        return jnp.where(keep, values, 0.0).astype(BF16)

    jd0, (rr0, dld0), lap_b = forward(0, b, lambda lap: [b * b, b * lap])
    back0, ww0 = backward(0, masked(jd0))
    alpha0 = rr0 / (ww0 + REG * dld0)
    x1 = alpha0 * b
    r1 = b - alpha0 * (back0 + REG * lap_b)

    jr1, (rr1, rlr, rld), lap_r = forward(1, r1, lambda lap: [r1 * r1, r1 * lap, r1 * lap_b])
    beta = rr1 / rr0
    back1, ww1 = backward(1, masked(jr1 + beta * jd0))
    dld1 = rlr + 2.0 * beta * rld + beta * beta * dld0
    alpha1 = rr1 / (ww1 + REG * dld1)
    d1 = r1 + beta * b
    x2 = x1 + alpha1 * d1
    r2 = r1 - alpha1 * (back1 + REG * (lap_r + beta * lap_b))
    for j in range(8):
        cols = slice((j % 4) * 128, (j % 4 + 1) * 128)
        upd[j // 4 : j // 4 + 1, cols] = x2[j : j + 1, :]
        res[j // 4 : j // 4 + 1, cols] = r2[j : j + 1, :]

    for it in range(2):
        drain(rs.at[it], rs_s.at[it])
        drain(rs.at[it], ag_s.at[it])
        drain(sc_rcv.at[it], sc_s.at[it])
    for phase in range(3):
        drain(zbuf.at[phase, pl.ds(0, PLANES - 1)], z_s.at[phase])
        drain(zsm.at[phase, pl.ds(0, PLANES - 1)], zsm_s.at[phase])


def on_device(source_field, detector_field, active_block_pairs, measurement_counts, measurement_residual):
    blocks = measurement_residual.reshape(PAIRS // 2, 2, BLOCK, BLOCK).transpose(0, 2, 1, 3)
    blocks = blocks.reshape(PAIRS // 2, BLOCK, 2 * BLOCK)
    dma = pltpu.SemaphoreType.DMA
    vmem = pltpu.VMEM
    out = jax.ShapeDtypeStruct((2, 512), F32)
    on_chip = pl.BlockSpec(memory_space=pltpu.VMEM)
    b_part, count_rows = pl.pallas_call(
        right_side_kernel,
        out_shape=(jax.ShapeDtypeStruct((8, 128), F32), jax.ShapeDtypeStruct((PLANES, 1, 128), F32)),
        in_specs=[pl.BlockSpec(memory_space=pltpu.SMEM)] * 2 + [on_chip] * 3,
        out_specs=(on_chip,) * 2,
        scratch_shapes=[vmem((8, 1024), F32)],
        compiler_params=pltpu.CompilerParams(vmem_limit_bytes=24 * 1024 * 1024),
    )(active_block_pairs, measurement_counts, source_field, detector_field, blocks)
    return pl.pallas_call(
        step_kernel,
        out_shape=(out, out),
        in_specs=[on_chip] * 4,
        out_specs=(on_chip,) * 2,
        scratch_shapes=[
            vmem((128, 1024), BF16),
            vmem((8, 1024), F32),
            vmem((2, 4, 128, 128), BF16),
            vmem((2, 4, 128, 128), BF16),
            vmem((4, 128, 128), F32),
            vmem((2, 4, 128, 128), BF16),
            vmem((2, CHIPS - 1, 16, 128), BF16),
            vmem((2, 8, 128, 128), BF16),
            vmem((2, 8, 128), F32),
            vmem((2, 2, 8, 128), F32),
            vmem((2, 1, 128), F32),
            vmem((2, 1, 128), F32),
            vmem((2, 1, 128), F32),
            vmem((2, CHIPS - 1, 1, 128), F32),
            vmem((3, PLANES, 8, 128), F32),
            vmem((3, PLANES, 1, 128), F32),
            dma((2, 2)), dma((2, 2)),
            dma((2,)), dma((2,)),
            dma((2,)), dma((2,)),
            dma((2,)), dma((2,)),
            dma((2,)), dma((2,)),
            dma((2,)), dma((2,)),
            dma((2,)), dma((2,)),
            dma((3,)), dma((3,)),
            dma((3,)), dma((3,)),
        ],
        compiler_params=pltpu.CompilerParams(
            collective_id=0, has_side_effects=True, vmem_limit_bytes=24 * 1024 * 1024
        ),
    )(source_field, detector_field, b_part, count_rows)


def solution(mesh):
    return jax.shard_map(
        on_device,
        mesh=mesh,
        in_specs=(P(None, "vox"), P(None, "vox"), P("grp", None), P("grp"), P("grp", None)),
        out_specs=(P("vox", None), P("vox", None)),
        check_vma=False,
    )
```
